128 devices in a mesh: store: 16 (over x, y), ctx: 8 (over z, core).
Axes of the slice: x: 4, y: 4, z: 4, core: 2. Of those that a mesh axis runs over, the one named last changes fastest.
Arguments:
- tokens: bfloat16 [2048, 8192], P('store'), may hold values from -6 to 6
- joined_weight: bfloat16 [8192, 8, 1280], P(None, 'ctx'), may hold values from -0.0625 to 0.0625
- down_weight: bfloat16 [128, 8192, 64], P('store', 'ctx'), may hold values from -0.0625 to 0.0625
- up_weight: bfloat16 [128, 64, 8, 1280], P('store', None, 'ctx'), may hold values from -0.75 to 0.75
- adapter_per_request: int32 [2048], replicated, may hold values from 0 to 127, as said below
- adapter_store_slot: int32 [128], replicated, may hold values from 0 to 127, as said below
- prefix_block_list: int32 [2048, 8], P('store'), may hold values from 0 to 255, as said below
- prefix_length: int32 [2048], P('store'), may hold values from 1 to 128, as said below
- key_value_pool: bfloat16 [4096, 8, 256], P(('store', 'ctx')), may hold values from -400 to 400
Outputs:
- attn: bfloat16 [2048, 8, 1024], P('store', 'ctx')
The draws below stay inside these ranges and needn't reach their ends.
Inputs may be any that keep to these rules, and one draw needn't show every extreme that they name: `adapter_store_slot`: A permutation; slot s belongs to owner s // 8, which holds slots in store order. `adapter_per_request`: among the 128 requests of one store shard, at most 16 use adapters of one owner; on every shard one owner, the same for all shards, receives exactly 16. `prefix_block_list`: the 8 blocks of a request are distinct and lie in its store shard's range of 16 blocks, rows i * 128 to (i+1) * 128 - 1 using blocks i * 16 to (i+1) * 16 - 1. `prefix_length`: every store shard has a request of length 128.
All inputs are finite; a program needn't handle non-finite values.
Results may differ from the reference program's by a relative error of at most 0.02.
The reference program's roundings to bfloat16 on the way count: a program that leaves them out, or rounds other values in their place, can miss the bound.
Values may be sent and summed in bfloat16 or wider, within the bound.
No kernel may reach another device: no remote copies, remote signals or barrier semaphores. Data moves between devices by JAX's collectives and lax.ppermute only.
A program may use at most 128 MiB of HBM per device.

```python
import jax
import jax.numpy as jnp
from jax import lax

MODEL_WIDTH = 8192
KEY_VALUE_HEADS = 8
QUERY_PER_KEY = 8
HEAD_SIZE = 128
ADAPTER_RANK = 64
CAP = 16
BLK = 16
SHARD_REQUESTS = 128
ADP_DEV = 8
REQUEST_COUNT = 2048
ADAPTER_COUNT = 128
GROUP_BLK = 16
MAXB = 8
MAXLEN = 128
PREFIX_TOKENS = 4096
JOINED_COLUMNS = 1280


def route_helper(key):
    shards = REQUEST_COUNT // SHARD_REQUESTS
    slot_of_adapter = jax.random.permutation(jax.random.fold_in(key, 11), ADAPTER_COUNT).astype(jnp.int32)
    adapter_of_slot = jnp.argsort(slot_of_adapter, stable=True).astype(jnp.int32)
    hot = jax.random.randint(jax.random.fold_in(key, 12), (), 0, shards)

    def one_shard(shard_key):
        initial_part, second, third = jax.random.split(shard_key, 3)
        positions = jnp.arange(shards * CAP, dtype=jnp.int32)
        ranks = jax.random.permutation(initial_part, shards * CAP).astype(jnp.int32) + CAP
        ranks = jnp.where(positions // CAP == hot, positions % CAP, ranks)
        chosen = jnp.argsort(ranks, stable=True)[:SHARD_REQUESTS].astype(jnp.int32)
        chosen = jax.random.permutation(second, chosen)
        owners = chosen // CAP
        local = jax.random.randint(third, (SHARD_REQUESTS,), 0, ADP_DEV)
        return adapter_of_slot[owners * ADP_DEV + local]
    keys = jax.random.split(jax.random.fold_in(key, 13), shards)
    request = jax.vmap(one_shard)(keys).reshape(REQUEST_COUNT)
    return (request.astype(jnp.int32), slot_of_adapter)


def draw_adapter_per_request(key, part):
    return route_helper(key)[0]


def draw_adapter_store_slot(key, part):
    return route_helper(key)[1]


def draw_prefix_block_list(key, part):
    keys = jax.random.split(key, REQUEST_COUNT)
    rows = jax.vmap(lambda row_key: jax.random.permutation(row_key, GROUP_BLK)[:MAXB])(keys)
    drawn_projection = jnp.arange(REQUEST_COUNT, dtype=jnp.int32) // SHARD_REQUESTS * GROUP_BLK
    return (rows.astype(jnp.int32) + drawn_projection[:, None]).astype(jnp.int32)


def draw_prefix_length(key, part):
    shards = REQUEST_COUNT // SHARD_REQUESTS
    initial_part, second = jax.random.split(key)
    lens = jax.random.randint(initial_part, (REQUEST_COUNT,), 1, MAXLEN + 1)
    where_long = jax.random.randint(second, (shards,), 0, SHARD_REQUESTS)
    index = jnp.arange(REQUEST_COUNT, dtype=jnp.int32)
    longest = index % SHARD_REQUESTS == jnp.repeat(where_long, SHARD_REQUESTS)
    return jnp.where(longest, MAXLEN, lens).astype(jnp.int32)


def draw_key_value_pool(key, part):
    initial_part = jax.random.fold_in(key, 0)
    value_rows = jnp.clip(jax.random.normal(initial_part, (PREFIX_TOKENS, KEY_VALUE_HEADS, 2 * HEAD_SIZE), jnp.float32), -6.0, 6.0)
    return value_rows.astype(jnp.bfloat16)


def steps_of(rng, dims, cuts, smallest, largest):
    loudness = 1.0
    for axis_at, parts in cuts:
        draws = jax.random.uniform(jax.random.fold_in(jax.random.fold_in(rng, 6), axis_at), (parts,), jnp.float32, smallest / len(cuts), largest / len(cuts))
        loudness = loudness * jnp.repeat(jnp.exp(draws), dims[axis_at] // parts).reshape((-1,) + (1,) * (len(dims) - 1 - axis_at))
    return loudness


def normal_values(key, shape, width, bound, cuts=(), kind=jnp.bfloat16):
    loudness = steps_of(key, shape, cuts, -0.22, 0.18) if cuts else 1.0
    drawn = jax.random.normal(key, shape, jnp.float32) * width * loudness
    return jnp.minimum(jnp.maximum(drawn, -bound), bound).astype(kind)


def setup_inputs(seed: int = 0) -> dict:
    seeds = jax.random.split(jax.random.key(seed), 10)
    tokens = normal_values(seeds[0], (REQUEST_COUNT, MODEL_WIDTH), 1.0, 6.0, ((0, 16),))
    joined_weight = normal_values(seeds[1], (MODEL_WIDTH, KEY_VALUE_HEADS, JOINED_COLUMNS), MODEL_WIDTH ** -0.5, 0.0625, ((1, 8),))
    down_weight = normal_values(seeds[2], (ADAPTER_COUNT, MODEL_WIDTH, ADAPTER_RANK), MODEL_WIDTH ** -0.5, 0.0625, ((0, 16), (1, 8)))
    up_weight = normal_values(seeds[3], (ADAPTER_COUNT, ADAPTER_RANK, KEY_VALUE_HEADS, JOINED_COLUMNS), ADAPTER_RANK ** -0.5, 0.75, ((0, 16), (2, 8)))
    adapter_per_request = draw_adapter_per_request(jax.random.fold_in(seeds[9], 71), 0)
    adapter_store_slot = draw_adapter_store_slot(jax.random.fold_in(seeds[9], 71), 0)
    prefix_block_list = draw_prefix_block_list(jax.random.fold_in(seeds[9], 71), 0)
    prefix_length = draw_prefix_length(jax.random.fold_in(seeds[9], 71), 0)
    key_value_pool = draw_key_value_pool(jax.random.fold_in(seeds[9], 71), 0)
    return {"tokens": tokens, "joined_weight": joined_weight, "down_weight": down_weight, "up_weight": up_weight, "adapter_per_request": adapter_per_request, "adapter_store_slot": adapter_store_slot, "prefix_block_list": prefix_block_list, "prefix_length": prefix_length, "key_value_pool": key_value_pool}


ROPE_THETA = 500000.0
ADAPTER_SCALE = 2.0


def rotary_apply(vec, token_position):
    half = vec.shape[-1] // 2
    freq = jnp.power(ROPE_THETA, -(jnp.arange(half, dtype=jnp.float32) * 2.0 / vec.shape[-1]))
    angle = token_position[..., None] * freq
    cosine = jnp.cos(angle)
    sine = jnp.sin(angle)
    initial_part = vec[..., :half]
    second = vec[..., half:]
    return jnp.concatenate([initial_part * cosine - second * sine, initial_part * sine + second * cosine], axis=-1)


def prefix_mask(local_ids, lens, group_blocks, blk):
    listed = local_ids.shape[1]
    equal = local_ids[:, :, None] == jnp.arange(group_blocks, dtype=jnp.int32)[None, None, :]
    start = jnp.sum(jnp.where(equal, (jnp.arange(listed, dtype=jnp.int32) * blk)[None, :, None], 0), axis=1)
    present = jnp.any(equal, axis=1)
    offset = jnp.arange(blk, dtype=jnp.int32)
    live = present[:, :, None] & (start[:, :, None] + offset[None, None, :] < lens[:, None, None])
    return live.reshape(local_ids.shape[0], group_blocks * blk)


def attend(query_rows, key_new, value_new, keys, value_rows, live):
    scale = 1.0 / (HEAD_SIZE ** 0.5)
    pool_scores = jnp.einsum('rhgd,thd->rhgt', query_rows.astype(jnp.float32), keys.astype(jnp.float32)) * scale
    own = jnp.einsum('rhgd,rhd->rhg', query_rows.astype(jnp.float32), key_new.astype(jnp.float32)) * scale
    mask = live[:, None, None, :]
    pool_scores = jnp.where(mask, pool_scores, -jnp.inf)
    top = jnp.maximum(jnp.max(pool_scores, axis=-1), own)
    prob = jnp.where(mask, jnp.exp(pool_scores - top[..., None]), 0.0)
    prob_own = jnp.exp(own - top)
    total = jnp.sum(prob, axis=-1) + prob_own
    prob_low = prob.astype(jnp.bfloat16)
    own_low = prob_own.astype(jnp.bfloat16)
    mixed = jnp.einsum('rhgt,thd->rhgd', prob_low.astype(jnp.float32), value_rows.astype(jnp.float32))
    mixed = mixed + own_low.astype(jnp.float32)[..., None] * value_new.astype(jnp.float32)[:, :, None, :]
    mixed = mixed / total[..., None]
    return mixed.astype(jnp.bfloat16).reshape(query_rows.shape[0], query_rows.shape[1], -1)


def reference(tokens, joined_weight, down_weight, up_weight, adapter_per_request, adapter_store_slot, prefix_block_list, prefix_length, key_value_pool):
    group_tokens = GROUP_BLK * BLK
    weight_flattened = joined_weight.reshape(MODEL_WIDTH, KEY_VALUE_HEADS * JOINED_COLUMNS)

    def one_shard(args):
        input_rows, adapters, lens, ids, shard = args
        store_slot = adapter_store_slot[adapters]
        down_picked = down_weight[store_slot].astype(jnp.float32)
        shrunk = jnp.einsum('rd,rdk->rk', input_rows.astype(jnp.float32), down_picked).astype(jnp.bfloat16)
        up_picked = up_weight[store_slot].astype(jnp.float32)
        adapter_update = jnp.einsum('rk,rkhc->rhc', shrunk.astype(jnp.float32), up_picked).astype(jnp.bfloat16)
        plain_projection = jnp.dot(input_rows, weight_flattened, preferred_element_type=jnp.float32).reshape(SHARD_REQUESTS, KEY_VALUE_HEADS, JOINED_COLUMNS)
        joined_projection = plain_projection + ADAPTER_SCALE * adapter_update.astype(jnp.float32)
        token_position = lens.astype(jnp.float32)
        query_rows = rotary_apply(joined_projection[:, :, :QUERY_PER_KEY * HEAD_SIZE].reshape(SHARD_REQUESTS, KEY_VALUE_HEADS, QUERY_PER_KEY, HEAD_SIZE), token_position[:, None, None]).astype(jnp.bfloat16)
        key_new = rotary_apply(joined_projection[:, :, QUERY_PER_KEY * HEAD_SIZE:(QUERY_PER_KEY + 1) * HEAD_SIZE], token_position[:, None]).astype(jnp.bfloat16)
        value_new = joined_projection[:, :, (QUERY_PER_KEY + 1) * HEAD_SIZE:].astype(jnp.bfloat16)
        group = lax.dynamic_slice_in_dim(key_value_pool, (shard * group_tokens).astype(jnp.int32), group_tokens, 0)
        live = prefix_mask(ids - (shard * GROUP_BLK).astype(jnp.int32), lens, GROUP_BLK, BLK)
        return attend(query_rows, key_new, value_new, group[:, :, :HEAD_SIZE], group[:, :, HEAD_SIZE:], live)

    shards = REQUEST_COUNT // SHARD_REQUESTS
    output_rows = lax.map(one_shard, (tokens.reshape(shards, SHARD_REQUESTS, MODEL_WIDTH), adapter_per_request.reshape(shards, SHARD_REQUESTS),
                                  prefix_length.reshape(shards, SHARD_REQUESTS), prefix_block_list.reshape(shards, SHARD_REQUESTS, MAXB),
                                  jnp.arange(shards, dtype=jnp.int32)))
    return output_rows.reshape(REQUEST_COUNT, KEY_VALUE_HEADS, QUERY_PER_KEY * HEAD_SIZE)
```

```python
import functools

import jax
import jax.numpy as jnp
import numpy as np
from jax import lax
from jax.experimental import pallas as pl
from jax.experimental.pallas import tpu as pltpu
from jax.sharding import PartitionSpec as P

QUERY_PER_KEY = 8
HEAD = 128
CAP = 16
BLK = 16
NZ = 4
ROPE_THETA = 500000.0
ADAPTER_SCALE = 2.0
BK = 512
STEPS_A = 8

F32 = jnp.float32
BF16 = jnp.bfloat16


def iota(shape, dim):
    return lax.broadcasted_iota(jnp.int32, shape, dim)


def before():
    return (iota((128, 128), 0) < iota((128, 128), 1)).astype(BF16)


def pack_kernel(adapter_ref, table_ref, tokens_ref, out_ref, dest_ref, x_ref, sem):
    shard = lax.axis_index("store")
    width = x_ref.shape[1]
    start = pl.multiple_of(lax.axis_index("ctx") * width, 128)
    copy = pltpu.make_async_copy(tokens_ref.at[:, pl.ds(start, width)], x_ref, sem)
    copy.start()
    shards = adapter_ref.shape[0]
    mine = jnp.broadcast_to(adapter_ref[pl.ds(shard, 1), :], (8, 128))
    table = jnp.broadcast_to(table_ref[...], (8, 128))
    slot = jnp.take_along_axis(table, mine, axis=1)[:1]
    owner = slot // 8
    hot = (owner == iota((shards, 128), 0)).astype(F32)
    counted = jnp.dot(hot.astype(BF16), before(), preferred_element_type=F32)
    rank = jnp.sum(hot * counted, axis=0, keepdims=True).astype(jnp.int32)
    dest = owner * CAP + rank
    dest_ref[...] = jnp.broadcast_to(dest, dest_ref.shape)
    place = (dest == iota((shards * CAP, 128), 0)).astype(F32).astype(BF16)
    copy.wait()
    out_ref[...] = jnp.dot(place, x_ref[...], preferred_element_type=F32).astype(BF16)


def first_kernel(adapter_ref, table_ref, pool_ref, x_ref, w_ref, acc_ref, local_ref, heads_ref):
    step = pl.program_id(0)

    @pl.when(step == 0)
    def _():
        shard = lax.axis_index("store")
        core = lax.axis_index("ctx") % 2
        shards = adapter_ref.shape[0]
        table = jnp.broadcast_to(table_ref[...], (shards, 128))
        slot = jnp.take_along_axis(table, adapter_ref[...], axis=1)
        sent = (slot // 8 == shard).astype(F32)
        rank = jnp.dot(sent.astype(BF16), before(), preferred_element_type=F32)
        rank = jnp.where(sent > 0, rank, -1.0)
        value = (slot % 8 + 1).astype(F32)
        position = iota((CAP, 128), 0).astype(F32)
        rows = [
            jnp.where(rank[h : h + 1] == position, value[h : h + 1], 0.0) for h in range(shards)
        ]
        column = jnp.sum(jnp.concatenate(rows, axis=0), axis=1, keepdims=True)
        n = shards * CAP
        square = jnp.where(iota((n, n), 0) == iota((n, n), 1), column, 0.0)
        local_ref[...] = jnp.broadcast_to(jnp.sum(square, axis=0, keepdims=True), local_ref.shape)
        row = iota((256, 256), 0)
        parity = jnp.where(row < 128, core, 1 - core)
        source = (row % 32) * 8 + ((row // 32) % NZ) * 2 + parity
        select = (source == iota((256, 256), 1)).astype(F32).astype(BF16)
        heads_ref[...] = jnp.dot(select, pool_ref[...], preferred_element_type=F32).astype(BF16)
        acc_ref[...] = jnp.zeros_like(acc_ref)

    acc_ref[...] += jnp.dot(x_ref[...], w_ref[...], preferred_element_type=F32)


def split_sum(x):
    high = x.astype(BF16)
    return high, (x - high.astype(F32)).astype(BF16)


def down_kernel(received_ref, down_ref, local_ref, heads_ref, part_ref, send_ref):
    every = lax.dot_general(
        down_ref[...], received_ref[...], (((1,), (1,)), ((), ())), preferred_element_type=F32
    )
    local = local_ref[:1]
    part = jnp.zeros(part_ref.shape, F32)
    for g in range(8):
        part = part + jnp.where(local == g + 1.0, every[g * 64 : (g + 1) * 64], 0.0)
    part_ref[...] = part
    high, low = split_sum(part)
    send_ref[:64] = high
    send_ref[64:128] = low
    send_ref[128:] = heads_ref[128:]


def middle_kernel(part_ref, heads_ref, other_ref, sum_ref, pool_ref, s1_ref, s2_ref, s3_ref):
    member = lax.axis_index("ctx")
    core = member % 2
    z = member // 2
    total = part_ref[...] + (other_ref[:64].astype(F32) + other_ref[64:128].astype(F32))
    sum_ref[...] = total
    high, low = split_sum(total)
    mine = pl.multiple_of(core * 32, 32)
    theirs = pl.multiple_of((1 - core) * 32, 32)
    for j, ref, base in ((0, pool_ref, 0), (1, s1_ref, 128), (2, s2_ref, 128), (3, s3_ref, 128)):
        at = pl.multiple_of(((z + j) % NZ) * 32, 32)
        ref[pl.ds(base + mine, 32), :] = heads_ref[pl.ds(at, 32), :]
        ref[pl.ds(base + theirs, 32), :] = other_ref[pl.ds(128 + at, 32), :]
        if j:
            ref[:64] = high
            ref[64:128] = low


def up_kernel(sum_ref, r1_ref, r2_ref, r3_ref, local_ref, up_ref, out_ref):
    total = sum_ref[...]
    for ref in (r1_ref, r2_ref, r3_ref):
        total = total + (ref[:64].astype(F32) + ref[64:128].astype(F32))
    shrunk = total.astype(BF16).astype(F32)
    local = local_ref[:1]
    spread = jnp.concatenate(
        [jnp.where(local == g + 1.0, shrunk, 0.0) for g in range(8)], axis=0
    ).astype(BF16)
    out_ref[...] = lax.dot_general(
        spread, up_ref[...], (((0,), (0,)), ((), ())), preferred_element_type=F32
    ).astype(BF16)


def second_kernel(acc_in_ref, x_ref, w_ref, dest_ref, ids_ref, lens_ref, tie_ref, acc_ref, place_ref, bias_ref):
    del tie_ref
    step = pl.program_id(0)

    @pl.when(step == 0)
    def _():
        acc_ref[...] = acc_in_ref[...]
        shard = lax.axis_index("store")
        z = lax.axis_index("ctx") // 2
        place = (dest_ref[:1] == iota((256, 128), 0)).astype(F32)
        place_ref[...] = place.T.astype(BF16)
        row = iota((256, 128), 0)
        block = ((z + NZ - row // 64) % NZ) * 4 + (row % 64) // BLK + shard * 16
        offset = row % BLK
        position = jnp.full((256, 128), 1 << 20, jnp.int32)
        for j in range(ids_ref.shape[0]):
            position = jnp.where(ids_ref[j : j + 1] == block, j * BLK + offset, position)
        bias = jnp.where(position < lens_ref[...], 0.0, -jnp.inf)
        bias_ref[...] = bias.T

    acc_ref[...] += jnp.dot(x_ref[...], w_ref[...], preferred_element_type=F32)


def attend_kernel(acc_ref, returned_ref, place_ref, bias_ref, cos_ref, sin_ref, p0_ref, r1_ref, r2_ref, r3_ref, out_ref):
    update = jnp.dot(place_ref[...], returned_ref[...], preferred_element_type=F32)
    joined = acc_ref[...] + ADAPTER_SCALE * update
    cosine = cos_ref[...]
    sine = sin_ref[...]

    def rope(v):
        return (v * cosine + pltpu.roll(v, HEAD // 2, 1) * sine).astype(BF16)

    key_new = rope(joined[:, 8 * HEAD : 9 * HEAD]).astype(F32)
    value_new = joined[:, 9 * HEAD :].astype(BF16).astype(F32)
    pool = jnp.concatenate([p0_ref[...], r1_ref[128:], r2_ref[128:], r3_ref[128:]], axis=0)
    keys = pool[:, :HEAD]
    values = pool[:, HEAD:]
    bias = bias_ref[...]
    scale = 1.0 / HEAD**0.5
    for g in range(QUERY_PER_KEY):
        query = rope(joined[:, g * HEAD : (g + 1) * HEAD])
        score = lax.dot_general(query, keys, (((1,), (1,)), ((), ())), preferred_element_type=F32)
        score = score * scale + bias
        own = jnp.sum(query.astype(F32) * key_new, axis=1, keepdims=True) * scale
        top = jnp.maximum(jnp.max(score, axis=1, keepdims=True), own)
        prob = jnp.exp(score - top)
        prob_own = jnp.exp(own - top)
        total = jnp.sum(prob, axis=1, keepdims=True) + prob_own
        mixed = jnp.dot(prob.astype(BF16), values, preferred_element_type=F32)
        mixed = mixed + prob_own.astype(BF16).astype(F32) * value_new
        out_ref[:, g * HEAD : (g + 1) * HEAD] = (mixed / total).astype(BF16)


def shapes(*pairs):
    return [jax.ShapeDtypeStruct(s, d) for s, d in pairs]


def call(kernel, out, cost, *args):
    return pl.pallas_call(
        kernel,
        out_shape=out,
        name=kernel.__name__,
        cost_estimate=pl.CostEstimate(flops=cost[0], bytes_accessed=cost[1], transcendentals=0),
        compiler_params=pltpu.CompilerParams(vmem_limit_bytes=16 << 20),
    )(*args)


def whole(shape):
    return pl.BlockSpec(shape, lambda i: (0,) * len(shape))


def body(
    tokens,
    joined_weight,
    down_weight,
    up_weight,
    adapter_per_request,
    adapter_store_slot,
    prefix_block_list,
    prefix_length,
    key_value_pool,
):
    n_store = lax.axis_size("store")
    n_ctx = lax.axis_size("ctx")
    requests, d_model = tokens.shape
    width = down_weight.shape[1]
    columns = joined_weight.shape[2]
    slots = n_store * CAP
    adapters = adapter_per_request.reshape(n_store, requests)
    table = adapter_store_slot.reshape(1, 128)
    weight = joined_weight.reshape(d_model, columns)
    down = down_weight.transpose(0, 2, 1).reshape(-1, width)
    up = up_weight.reshape(-1, columns)
    pool = key_value_pool.reshape(-1, 2 * HEAD)

    outgoing, dest = pl.pallas_call(
        pack_kernel,
        out_shape=shapes(((slots, width), BF16), ((8, 128), jnp.int32)),
        name="pack_kernel",
        in_specs=[
            pl.BlockSpec(memory_space=pltpu.VMEM),
            pl.BlockSpec(memory_space=pltpu.VMEM),
            pl.BlockSpec(memory_space=pl.ANY),
        ],
        scratch_shapes=[pltpu.VMEM((requests, width), BF16), pltpu.SemaphoreType.DMA],
        cost_estimate=pl.CostEstimate(flops=1 << 26, bytes_accessed=1 << 20, transcendentals=0),
        compiler_params=pltpu.CompilerParams(vmem_limit_bytes=16 << 20),
    )(adapters, table, tokens)

    received = lax.all_to_all(
        outgoing.reshape(n_store, CAP, width), "store", split_axis=0, concat_axis=0, tiled=True
    ).reshape(slots, width)

    steps = d_model // BK
    acc, local, heads = pl.pallas_call(
        first_kernel,
        grid=(STEPS_A,),
        out_shape=shapes(((requests, columns), F32), ((8, slots), F32), ((256, 256), BF16)),
        name="first_kernel",
        in_specs=[
            whole(adapters.shape),
            whole(table.shape),
            whole(pool.shape),
            pl.BlockSpec((requests, BK), lambda i: (0, i)),
            pl.BlockSpec((BK, columns), lambda i: (i, 0)),
        ],
        out_specs=[whole((requests, columns)), whole((8, slots)), whole((256, 256))],
        cost_estimate=pl.CostEstimate(
            flops=2 * requests * columns * BK * STEPS_A,
            bytes_accessed=2 * BK * STEPS_A * columns,
            transcendentals=0,
        ),
        compiler_params=pltpu.CompilerParams(vmem_limit_bytes=16 << 20),
    )(adapters, table, pool, tokens, weight)

    part, send = call(
        down_kernel,
        shapes(((64, slots), F32), ((256, 256), BF16)),
        (1 << 28, 1 << 21),
        received,
        down,
        local,
        heads,
    )
    other = lax.ppermute(send, "ctx", [(i, i ^ 1) for i in range(n_ctx)])
    total, pool0, s1, s2, s3 = call(
        middle_kernel,
        shapes(((64, slots), F32), ((64, 256), BF16), *[((192, 256), BF16)] * 3),
        (1 << 16, 1 << 19),
        part,
        heads,
        other,
    )
    r1, r2, r3 = [
        lax.ppermute(s, "ctx", [(i, (i + 2 * j) % n_ctx) for i in range(n_ctx)])
        for j, s in ((1, s1), (2, s2), (3, s3))
    ]
    update = call(
        up_kernel,
        shapes(((slots, columns), BF16))[0],
        (1 << 28, 1 << 21),
        total,
        r1,
        r2,
        r3,
        local,
        up,
    )
    returned = lax.all_to_all(
        update.reshape(n_store, CAP, columns), "store", split_axis=0, concat_axis=0, tiled=True
    ).reshape(slots, columns)

    acc, place, bias = pl.pallas_call(
        second_kernel,
        grid=(steps - STEPS_A,),
        out_shape=shapes(((requests, columns), F32), ((requests, slots), BF16), ((requests, 256), F32)),
        name="second_kernel",
        in_specs=[
            whole((requests, columns)),
            pl.BlockSpec((requests, BK), lambda i: (0, STEPS_A + i)),
            pl.BlockSpec((BK, columns), lambda i: (STEPS_A + i, 0)),
            whole((8, 128)),
            whole((8, 128)),
            whole((1, 128)),
            pl.BlockSpec((16, 128), lambda i: (0, 0)),
        ],
        out_specs=[whole((requests, columns)), whole((requests, slots)), whole((requests, 256))],
        input_output_aliases={0: 0},
        cost_estimate=pl.CostEstimate(
            flops=2 * requests * columns * BK * (steps - STEPS_A),
            bytes_accessed=2 * BK * (steps - STEPS_A) * columns,
            transcendentals=0,
        ),
        compiler_params=pltpu.CompilerParams(vmem_limit_bytes=16 << 20),
    )(acc, tokens, weight, dest, prefix_block_list.T, prefix_length.reshape(1, requests), update)

    frequency = np.power(
        np.float32(ROPE_THETA), -(np.arange(HEAD // 2, dtype=np.float32) * np.float32(2.0 / HEAD))
    ).astype(np.float32)
    angle = prefix_length.astype(F32)[:, None] * jnp.asarray(np.tile(frequency, 2))[None, :]
    cosine = jnp.cos(angle)
    sine = jnp.sin(angle) * jnp.asarray(np.repeat(np.float32([-1.0, 1.0]), HEAD // 2))[None, :]

    out = call(
        attend_kernel,
        shapes(((requests, QUERY_PER_KEY * HEAD), BF16))[0],
        (1 << 28, 1 << 21),
        acc,
        returned,
        place,
        bias,
        cosine,
        sine,
        pool0,
        r1,
        r2,
        r3,
    )
    return out.reshape(requests, 1, QUERY_PER_KEY * HEAD)


def solution(mesh):
    in_specs = (
        P("store", None),
        P(None, "ctx", None),
        P("store", "ctx", None),
        P("store", None, "ctx", None),
        P(),
        P(),
        P("store", None),
        P("store"),
        P(("store", "ctx"), None, None),
    )
    out_specs = P("store", "ctx", None)
    return jax.shard_map(body, mesh=mesh, in_specs=in_specs, out_specs=out_specs, check_vma=False)
```

```python
import jax
import jax.numpy as jnp
import numpy as np
from jax import lax
from jax.experimental import pallas as pl
from jax.experimental.pallas import tpu as pltpu
from jax.sharding import PartitionSpec as P

QUERY_PER_KEY = 8
HEAD = 128
CAP = 16
BLK = 16
NZ = 4
ROPE_THETA = 500000.0
ADAPTER_SCALE = 2.0
BK = 512
AHEAD = 4
STEPS_A = 8

F32 = jnp.float32
BF16 = jnp.bfloat16


def iota(shape, dim):
    return lax.broadcasted_iota(jnp.int32, shape, dim)


def before():
    return (iota((128, 128), 0) < iota((128, 128), 1)).astype(BF16)


def pack_kernel(adapter_hbm, table_hbm, tokens_hbm, out_ref, dest_ref, adapter_ref, table_ref, x_ref, sems):
    shard = lax.axis_index("store")
    width = x_ref.shape[1]
    start = pl.multiple_of(lax.axis_index("ctx") * width, 128)
    copies = [
        pltpu.make_async_copy(adapter_hbm, adapter_ref, sems.at[0]),
        pltpu.make_async_copy(table_hbm, table_ref, sems.at[1]),
        pltpu.make_async_copy(tokens_hbm.at[:, pl.ds(start, width)], x_ref, sems.at[2]),
    ]
    for copy in copies:
        copy.start()
    copies[0].wait()
    copies[1].wait()
    shards = adapter_ref.shape[0]
    mine = jnp.broadcast_to(adapter_ref[pl.ds(shard, 1), :], (8, 128))
    table = jnp.broadcast_to(table_ref[...], (8, 128))
    slot = jnp.take_along_axis(table, mine, axis=1)[:1]
    owner = slot // 8
    hot = (owner == iota((shards, 128), 0)).astype(F32)
    counted = jnp.dot(hot.astype(BF16), before(), preferred_element_type=F32)
    rank = jnp.sum(hot * counted, axis=0, keepdims=True).astype(jnp.int32)
    dest = owner * CAP + rank
    dest_ref[...] = jnp.broadcast_to(dest, dest_ref.shape)
    place = (dest == iota((shards * CAP, 128), 0)).astype(F32).astype(BF16)
    copies[2].wait()
    out_ref[...] = jnp.dot(place, x_ref[...], preferred_element_type=F32).astype(BF16)


def stream(x_hbm, w_hbm, x_ref, w_ref, sems, first, steps):
    copies = []
    for i in range(steps):
        here = pl.ds(i * BK, BK)
        there = pl.ds((first + i) * BK, BK)
        copies.append(
            (
                pltpu.make_async_copy(x_hbm.at[:, there], x_ref.at[:, here], sems.at[i, 0]),
                pltpu.make_async_copy(w_hbm.at[there, :], w_ref.at[here, :], sems.at[i, 1]),
            )
        )
    for pair in copies[:AHEAD]:
        for copy in pair:
            copy.start()
    return copies


def multiply(copies, acc_ref, x_ref, w_ref):
    for i, pair in enumerate(copies):
        for copy in pair:
            copy.wait()
        if i + AHEAD < len(copies):
            for copy in copies[i + AHEAD]:
                copy.start()
        rows = slice(i * BK, (i + 1) * BK)
        acc_ref[...] += jnp.dot(x_ref[:, rows], w_ref[rows, :], preferred_element_type=F32)


def first_kernel(
    adapter_hbm, table_hbm, pool_hbm, x_hbm, w_hbm,
    acc_ref, local_ref, heads_ref,
    adapter_ref, table_ref, pool_ref, x_ref, w_ref, sems, more,
):
    small = [
        pltpu.make_async_copy(adapter_hbm, adapter_ref, more.at[0]),
        pltpu.make_async_copy(table_hbm, table_ref, more.at[1]),
        pltpu.make_async_copy(pool_hbm, pool_ref, more.at[2]),
    ]
    for copy in small:
        copy.start()
    copies = stream(x_hbm, w_hbm, x_ref, w_ref, sems, 0, STEPS_A)
    for copy in small:
        copy.wait()
    shard = lax.axis_index("store")
    core = lax.axis_index("ctx") % 2
    shards = adapter_ref.shape[0]
    table = jnp.broadcast_to(table_ref[...], (shards, 128))
    slot = jnp.take_along_axis(table, adapter_ref[...], axis=1)
    sent = (slot // 8 == shard).astype(F32)
    rank = jnp.dot(sent.astype(BF16), before(), preferred_element_type=F32)
    rank = jnp.where(sent > 0, rank, -1.0)
    value = (slot % 8 + 1).astype(F32)
    position = iota((CAP, 128), 0).astype(F32)
    rows = [jnp.where(rank[h : h + 1] == position, value[h : h + 1], 0.0) for h in range(shards)]
    column = jnp.sum(jnp.concatenate(rows, axis=0), axis=1, keepdims=True)
    local_ref[...] = jnp.broadcast_to(column, local_ref.shape)
    row = iota((256, 256), 0)
    parity = jnp.where(row < 128, core, 1 - core)
    source = (row % 32) * 8 + ((row // 32) % NZ) * 2 + parity
    select = (source == iota((256, 256), 1)).astype(F32).astype(BF16)
    heads_ref[...] = jnp.dot(select, pool_ref[...], preferred_element_type=F32).astype(BF16)
    acc_ref[...] = jnp.zeros_like(acc_ref)
    multiply(copies, acc_ref, x_ref, w_ref)


def split_sum(x):
    high = x.astype(BF16).astype(F32)
    return jnp.where(iota(x.shape, 1) < 64, high, x - high).astype(BF16)


def join_sum(x):
    x = x.astype(F32)
    return x + pltpu.roll(x, 64, 1)


def down_kernel(received_ref, down_ref, local_ref, heads_ref, part_ref, send_ref):
    every = lax.dot_general(
        received_ref[...], down_ref[...], (((1,), (1,)), ((), ())), preferred_element_type=F32
    )
    local = local_ref[...]
    half = (iota(local.shape, 1) // 64).astype(F32)
    part = jnp.zeros(local.shape, F32)
    for m in range(4):
        part = part + jnp.where(local == 2.0 * m + 1.0 + half, every[:, m * 128 : (m + 1) * 128], 0.0)
    part = part + pltpu.roll(part, 64, 1)
    part_ref[...] = part
    send_ref[:256] = split_sum(part)
    send_ref[256:384] = heads_ref[128:, :HEAD]
    send_ref[384:] = heads_ref[128:, HEAD:]


def middle_kernel(part_ref, heads_ref, other_ref, sum_ref, pool_ref, s1_ref, s2_ref, s3_ref):
    member = lax.axis_index("ctx")
    core = member % 2
    z = member // 2
    total = part_ref[...] + join_sum(other_ref[:256])
    sum_ref[...] = total
    both = split_sum(total)
    mine = pl.multiple_of(core * 32, 32)
    theirs = pl.multiple_of((1 - core) * 32, 32)
    for j, ref, base in ((0, pool_ref, 0), (1, s1_ref, 256), (2, s2_ref, 256), (3, s3_ref, 256)):
        at = pl.multiple_of(((z + j) % NZ) * 32, 32)
        for side in range(2):
            to = base + 64 * side
            columns = slice(side * HEAD, (side + 1) * HEAD)
            ref[pl.ds(to + mine, 32), :] = heads_ref[pl.ds(at, 32), columns]
            ref[pl.ds(to + theirs, 32), :] = other_ref[pl.ds(256 + 128 * side + at, 32), :]
        if j:
            ref[:256] = both


def up_kernel(sum_ref, r1_ref, r2_ref, r3_ref, local_ref, up_ref, out_ref):
    total = sum_ref[...]
    for ref in (r1_ref, r2_ref, r3_ref):
        total = total + join_sum(ref[:256])
    shrunk = total.astype(BF16).astype(F32)
    local = local_ref[...]
    half = (iota(local.shape, 1) // 64).astype(F32)
    spread = jnp.concatenate(
        [jnp.where(local == 2.0 * m + 1.0 + half, shrunk, 0.0).astype(BF16) for m in range(4)], axis=1
    )
    out_ref[...] = jnp.dot(spread, up_ref[...], preferred_element_type=F32).astype(BF16)


ACC = slice(0, 1280)
BIAS = slice(1280, 1536)
COS = slice(1536, 1664)
SIN = slice(1664, 1792)
DEST = slice(1792, 1920)
POOL = 1920
AUX = 2432


def second_kernel(
    acc_hbm, dest_ref, ids_hbm, lens_hbm, cos_ref, sin_ref, x_hbm, w_hbm, p0_ref, r1_ref, r2_ref, r3_ref, tie_ref,
    aux_ref,
    ids_ref, lens_ref, acc_ref, x_ref, w_ref, sems, more,
):
    del tie_ref
    small = [
        pltpu.make_async_copy(ids_hbm, ids_ref, more.at[0]),
        pltpu.make_async_copy(lens_hbm, lens_ref, more.at[1]),
        pltpu.make_async_copy(acc_hbm, acc_ref, more.at[2]),
    ]
    for copy in small:
        copy.start()
    copies = stream(x_hbm, w_hbm, x_ref, w_ref, sems, STEPS_A, sems.shape[0])
    aux_ref[:, DEST] = jnp.broadcast_to(dest_ref[:1].astype(F32), (128, 128)).T
    cosine = cos_ref[...]
    sine = sin_ref[...]
    aux_ref[:, COS] = jnp.concatenate([cosine, cosine], axis=1)
    aux_ref[:, SIN] = jnp.concatenate([-sine, sine], axis=1)
    for i, (ref, at) in enumerate(((p0_ref, 0), (r1_ref, 256), (r2_ref, 256), (r3_ref, 256))):
        rows = slice(64 * (i % 2), 64 * (i % 2) + 64)
        column = POOL + 256 * (i // 2)
        aux_ref[rows, column : column + 128] = ref[at : at + 64].astype(F32)
        aux_ref[rows, column + 128 : column + 256] = ref[at + 64 : at + 128].astype(F32)
    small[0].wait()
    small[1].wait()
    shard = lax.axis_index("store")
    z = lax.axis_index("ctx") // 2
    row = iota((256, 128), 0)
    block = ((z + NZ - row // 64) % NZ) * 4 + (row % 64) // BLK + shard * 16
    offset = row % BLK
    position = jnp.full((256, 128), 1 << 20, jnp.int32)
    for j in range(ids_ref.shape[0]):
        position = jnp.where(ids_ref[j : j + 1] == block, j * BLK + offset, position)
    aux_ref[:, BIAS] = jnp.where(position < lens_ref[...], 0.0, -jnp.inf).T
    small[2].wait()
    multiply(copies, acc_ref, x_ref, w_ref)
    aux_ref[:, ACC] = acc_ref[...]


def attend_kernel(aux_ref, returned_ref, out_ref):
    slots = returned_ref.shape[0]
    dest = aux_ref[:, DEST]
    dest = jnp.concatenate([dest] * (slots // 128), axis=1)
    place = (dest == iota(dest.shape, 1).astype(F32)).astype(F32).astype(BF16)
    update = jnp.dot(place, returned_ref[...], preferred_element_type=F32)
    joined = aux_ref[:, ACC] + ADAPTER_SCALE * update
    cosine = aux_ref[:, COS]
    sine = aux_ref[:, SIN]

    def rope(v):
        return (v * cosine + pltpu.roll(v, HEAD // 2, 1) * sine).astype(BF16)

    key_new = rope(joined[:, 8 * HEAD : 9 * HEAD]).astype(F32)
    value_new = joined[:, 9 * HEAD :].astype(BF16).astype(F32)
    keys = jnp.concatenate([aux_ref[:, POOL + c : POOL + c + 128] for c in (0, 256)], axis=0).astype(BF16)
    values = jnp.concatenate([aux_ref[:, POOL + c : POOL + c + 128] for c in (128, 384)], axis=0).astype(BF16)
    bias = aux_ref[:, BIAS]
    scale = 1.0 / HEAD**0.5
    for g in range(QUERY_PER_KEY):
        query = rope(joined[:, g * HEAD : (g + 1) * HEAD])
        score = lax.dot_general(query, keys, (((1,), (1,)), ((), ())), preferred_element_type=F32)
        score = score * scale + bias
        own = jnp.sum(query.astype(F32) * key_new, axis=1, keepdims=True) * scale
        top = jnp.maximum(jnp.max(score, axis=1, keepdims=True), own)
        prob = jnp.exp(score - top)
        prob_own = jnp.exp(own - top)
        total = jnp.sum(prob, axis=1, keepdims=True) + prob_own
        mixed = jnp.dot(prob.astype(BF16), values, preferred_element_type=F32)
        mixed = mixed + prob_own.astype(BF16).astype(F32) * value_new
        out_ref[:, g * HEAD : (g + 1) * HEAD] = (mixed / total).astype(BF16)


def shapes(*pairs):
    return [jax.ShapeDtypeStruct(s, d) for s, d in pairs]


HBM = pl.BlockSpec(memory_space=pltpu.HBM)
VMEM = pl.BlockSpec(memory_space=pltpu.VMEM)


def call(kernel, out, cost, *args, ins=None, scratch=(), vmem=8):
    return pl.pallas_call(
        kernel,
        out_shape=out,
        name=kernel.__name__,
        in_specs=ins or [VMEM] * len(args),
        scratch_shapes=scratch,
        cost_estimate=pl.CostEstimate(flops=int(cost[0]*1), bytes_accessed=int(cost[1]*1), transcendentals=0),
        compiler_params=pltpu.CompilerParams(vmem_limit_bytes=vmem << 20),
    )(*args)


def body(
    tokens,
    joined_weight,
    down_weight,
    up_weight,
    adapter_per_request,
    adapter_store_slot,
    prefix_block_list,
    prefix_length,
    key_value_pool,
):
    n_store = lax.axis_size("store")
    n_ctx = lax.axis_size("ctx")
    requests, d_model = tokens.shape
    width = down_weight.shape[1]
    columns = joined_weight.shape[2]
    slots = n_store * CAP
    adapters = adapter_per_request.reshape(n_store, requests)
    table = adapter_store_slot.reshape(1, 128)
    weight = joined_weight.reshape(d_model, columns)
    down = down_weight.transpose(0, 2, 1).reshape(-1, width)
    up = up_weight.reshape(-1, columns)
    pool = key_value_pool.reshape(-1, 2 * HEAD)
    tokens, weight, adapters, table, pool = [
        pltpu.with_memory_space_constraint(a, pltpu.HBM) for a in (tokens, weight, adapters, table, pool)
    ]
    small = [pltpu.VMEM(adapters.shape, jnp.int32), pltpu.VMEM(table.shape, jnp.int32)]

    outgoing, dest = call(
        pack_kernel,
        shapes(((slots, width), BF16), ((8, 128), jnp.int32)),
        (1 << 26, 1 << 20),
        adapters,
        table,
        tokens,
        ins=[HBM] * 3,
        vmem=8,
        scratch=[*small, pltpu.VMEM((requests, width), BF16), pltpu.SemaphoreType.DMA((3,))],
    )
    received = lax.all_to_all(
        outgoing.reshape(n_store, CAP, width), "store", split_axis=0, concat_axis=0, tiled=True
    ).reshape(slots, width)

    def parts(steps):
        return [
            pltpu.VMEM((requests, steps * BK), BF16),
            pltpu.VMEM((steps * BK, columns), BF16),
            pltpu.SemaphoreType.DMA((steps, 2)),
            pltpu.SemaphoreType.DMA((4,)),
        ]

    def cost(steps):
        return (2 * requests * columns * BK * steps, 2 * BK * steps * columns)

    acc, local, heads = call(
        first_kernel,
        shapes(((requests, columns), F32), ((slots, 128), F32), ((256, 256), BF16)),
        cost(STEPS_A),
        adapters,
        table,
        pool,
        tokens,
        weight,
        ins=[HBM] * 5,
        scratch=[*small, pltpu.VMEM(pool.shape, BF16), *parts(STEPS_A)],
        vmem=24,
    )
    acc = pltpu.with_memory_space_constraint(acc, pltpu.HBM)
    part, send = call(
        down_kernel,
        shapes(((slots, 128), F32), ((512, 128), BF16)),
        (1 << 28, 1 << 21),
        received,
        down,
        local,
        heads,
        vmem=8,
    )
    other = lax.ppermute(send, "ctx", [(i, i ^ 1) for i in range(n_ctx)])
    total, pool0, s1, s2, s3 = call(
        middle_kernel,
        shapes(((slots, 128), F32), ((128, 128), BF16), *[((384, 128), BF16)] * 3),
        (1 << 16, 1 << 19),
        part,
        heads,
        other,
        vmem=8,
    )
    r1, r2, r3 = [
        lax.ppermute(s, "ctx", [(i, (i + 2 * j) % n_ctx) for i in range(n_ctx)])
        for j, s in ((1, s1), (2, s2), (3, s3))
    ]
    update = call(
        up_kernel,
        shapes(((slots, columns), BF16))[0],
        (1 << 28, 1 << 21),
        total,
        r1,
        r2,
        r3,
        local,
        up,
        vmem=8,
    )
    returned = lax.all_to_all(
        update.reshape(n_store, CAP, columns), "store", split_axis=0, concat_axis=0, tiled=True
    ).reshape(slots, columns)

    frequency = np.power(
        np.float32(ROPE_THETA), -(np.arange(HEAD // 2, dtype=np.float32) * np.float32(2.0 / HEAD))
    ).astype(np.float32)
    angle = prefix_length.astype(F32)[:, None] * jnp.asarray(frequency)[None, :]
    rest = d_model // BK - STEPS_A
    ids = prefix_block_list.T
    lens = prefix_length.reshape(1, requests)
    aux = call(
        second_kernel,
        shapes(((requests, AUX), F32))[0],
        cost(rest),
        acc,
        dest,
        ids,
        lens,
        jnp.cos(angle),
        jnp.sin(angle),
        tokens,
        weight,
        pool0,
        r1,
        r2,
        r3,
        update,
        ins=[HBM, VMEM, HBM, HBM, VMEM, VMEM, HBM, HBM, VMEM, VMEM, VMEM, VMEM, pl.BlockSpec(memory_space=pl.ANY)],
        scratch=[
            pltpu.VMEM(ids.shape, jnp.int32),
            pltpu.VMEM(lens.shape, jnp.int32),
            pltpu.VMEM((requests, columns), F32),
            *parts(rest),
        ],
        vmem=24,
    )
    out = call(
        attend_kernel,
        shapes(((requests, QUERY_PER_KEY * HEAD), BF16))[0],
        (1 << 28, 1 << 21),
        aux,
        returned,
        vmem=8,
    )
    return out.reshape(requests, 1, QUERY_PER_KEY * HEAD)


def solution(mesh):
    in_specs = (
        P("store", None),
        P(None, "ctx", None),
        P("store", "ctx", None),
        P("store", None, "ctx", None),
        P(),
        P(),
        P("store", None),
        P("store"),
        P(("store", "ctx"), None, None),
    )
    out_specs = P("store", "ctx", None)
    return jax.shard_map(body, mesh=mesh, in_specs=in_specs, out_specs=out_specs, check_vma=False)
```
